32 devices in a mesh: section: 2 (over y), dp: 16 (over z, x, core).
Axes of the slice: x: 2, y: 2, z: 4, core: 2. Of those that a mesh axis runs over, the one named last changes fastest.
Arguments:
- inputs: bfloat16 [32, 128, 640], P('dp'), may hold values from -6 to 6
- lengths: int32 [32], P('dp'), may hold values from 16 to 128, as said below
- cotangent: bfloat16 [32, 128, 640], P('dp'), may hold values from -6 to 6
- ln1_gain: bfloat16 [2, 640], P('section', 'dp'), may hold values from 0.5 to 1.5
- ln1_bias: bfloat16 [2, 640], P('section', 'dp'), may hold values from -1.75 to 1.75
- w_query: bfloat16 [2, 640, 640], P('section', 'dp'), may hold values from -0.5 to 0.5
- b_query: bfloat16 [2, 640], P('section', 'dp'), may hold values from -3 to 3
- w_key: bfloat16 [2, 640, 640], P('section', 'dp'), may hold values from -0.25 to 0.25
- w_value: bfloat16 [2, 640, 640], P('section', 'dp'), may hold values from -0.25 to 0.25
- b_value: bfloat16 [2, 640], P('section', 'dp'), may hold values from -3 to 3
- w_out: bfloat16 [2, 640, 640], P('section', 'dp'), may hold values from -2.5 to 2.5
- b_out: bfloat16 [2, 640], P('section', 'dp'), may hold values from -3 to 3
- ln2_gain: bfloat16 [2, 640], P('section', 'dp'), may hold values from 0.5 to 1.5
- ln2_bias: bfloat16 [2, 640], P('section', 'dp'), may hold values from -1.75 to 1.75
- w_inner: bfloat16 [2, 640, 5120], P('section', 'dp'), may hold values from -0.25 to 0.25
- b_inner: bfloat16 [2, 5120], P('section', 'dp'), may hold values from -3 to 3
- w_outer: bfloat16 [2, 5120, 640], P('section', 'dp'), may hold values from -0.078125 to 0.078125
- b_outer: bfloat16 [2, 640], P('section', 'dp'), may hold values from -3 to 3
Outputs:
- layer_out: bfloat16 [2, 32, 128, 640], P('section', 'dp')
- input_grads: bfloat16 [2, 32, 128, 640], P('section', 'dp')
- ln1_gain_grad: float32 [2, 640], P('section', 'dp')
- ln1_bias_grad: float32 [2, 640], P('section', 'dp')
- w_query_grad: float32 [2, 640, 640], P('section', 'dp')
- b_query_grad: float32 [2, 640], P('section', 'dp')
- w_key_grad: float32 [2, 640, 640], P('section', 'dp')
- w_value_grad: float32 [2, 640, 640], P('section', 'dp')
- b_value_grad: float32 [2, 640], P('section', 'dp')
- w_out_grad: float32 [2, 640, 640], P('section', 'dp')
- b_out_grad: float32 [2, 640], P('section', 'dp')
- ln2_gain_grad: float32 [2, 640], P('section', 'dp')
- ln2_bias_grad: float32 [2, 640], P('section', 'dp')
- w_inner_grad: float32 [2, 640, 5120], P('section', 'dp')
- b_inner_grad: float32 [2, 5120], P('section', 'dp')
- w_outer_grad: float32 [2, 5120, 640], P('section', 'dp')
- b_outer_grad: float32 [2, 640], P('section', 'dp')
The draws below stay inside these ranges and needn't reach their ends.
Inputs may be any that keep to these rules, and one draw needn't show every extreme that they name: `lengths`: one sequence has exactly 128 real nucleotides.
All inputs are finite; a program needn't handle non-finite values.
Results may differ from the reference program's by a relative error of at most 0.019.
Values may be sent and summed in bfloat16 or wider, within the bound.
No kernel may reach another device: no remote copies, remote signals or barrier semaphores. Data moves between devices by JAX's collectives and lax.ppermute only.
A program may use at most 192 MiB of HBM per device.

```python
import math
import jax
import jax.numpy as jnp
from jax import lax

D = 640
HEADS = 20
HEAD_DIM = 32
FF = 5120
LEN = 128
SEQS = 32


def draw_lengths(key, part):
    first_key, second_key = jax.random.split(key)
    chosen_lengths = jax.random.randint(first_key, (SEQS,), LEN // 8, LEN + 1)
    longest = jax.random.randint(second_key, (), 0, SEQS)
    return chosen_lengths.at[longest].set(LEN).astype(jnp.int32)


def spiked(drawn, key, source, target, parts, factor):
    owner, partner = [(jnp.arange(drawn.shape[dim]) // (drawn.shape[dim] // parts)).reshape([-1 if axis == dim else 1 for axis in range(drawn.ndim)]) for dim in (source, target)]
    chosen = jax.random.permutation(key, parts)[partner]
    strong = (owner == chosen) | (owner == (partner + parts // 2) % parts)
    return jnp.where(strong, factor * drawn, drawn)


def block_scale(key, shape, cuts, low, largest):
    gain = 1.0
    for axis_at, blocks in cuts:
        draws = jax.random.uniform(jax.random.fold_in(jax.random.fold_in(key, 6), axis_at), (blocks,), jnp.float32, low / len(cuts), largest / len(cuts))
        gain = gain * jnp.repeat(jnp.exp(draws), shape[axis_at] // blocks).reshape((-1,) + (1,) * (len(shape) - 1 - axis_at))
    return gain


def scatter_about(own_key, dims, spread, limit, cuts=(), kind=jnp.bfloat16):
    result = spread * jax.random.normal(own_key, dims, jnp.float32)
    if cuts:
        result = result * block_scale(own_key, dims, cuts, -0.22, 0.18)
    return jnp.clip(result, -limit, limit).astype(kind)


def heavy_noise(key, extent, spread, bound, cuts, heavy, held_as=jnp.bfloat16):
    values = spread * jax.random.normal(key, extent, jnp.float32)
    if cuts:
        values = values * block_scale(key, extent, cuts, -0.22, 0.18)
    return jnp.clip(spiked(values, jax.random.fold_in(key, 3), *heavy), -bound, bound).astype(held_as)


def setup_inputs(seed: int = 0) -> dict:
    keys = jax.random.split(jax.random.key(seed), 19)
    return {
        "inputs": heavy_noise(keys[0], (SEQS, LEN, D), 1.0, 6.0, ((0, 16),), (0, 2, 16, 2.0)),
        "lengths": draw_lengths(jax.random.fold_in(keys[18], 71), 0),
        "cotangent": scatter_about(keys[2], (SEQS, LEN, D), 1.0, 6.0, ((0, 16),)),
        "ln1_gain": jnp.clip(1.0 + 0.1 * jax.random.normal(keys[3], (2, D), jnp.float32), 0.5, 1.5).astype(jnp.bfloat16),
        "ln1_bias": scatter_about(keys[4], (2, D), 0.3, 1.75, ((0, 2), (1, 16))),
        "w_query": scatter_about(keys[5], (2, D, D), (D // 4) ** -0.5, 0.5, ((0, 2), (1, 16))),
        "b_query": scatter_about(keys[6], (2, D), 0.5, 3.0, ((0, 2), (1, 16))),
        "w_key": scatter_about(keys[7], (2, D, D), D ** -0.5, 0.25, ((0, 2), (1, 16))),
        "w_value": scatter_about(keys[8], (2, D, D), D ** -0.5, 0.25, ((0, 2), (1, 16))),
        "b_value": scatter_about(keys[9], (2, D), 0.5, 3.0, ((0, 2), (1, 16))),
        "w_out": scatter_about(keys[10], (2, D, D), (D // 128) ** -0.5, 2.5, ((0, 2), (1, 16))),
        "b_out": scatter_about(keys[11], (2, D), 0.5, 3.0, ((0, 2), (1, 16))),
        "ln2_gain": jnp.clip(1.0 + 0.1 * jax.random.normal(keys[12], (2, D), jnp.float32), 0.5, 1.5).astype(jnp.bfloat16),
        "ln2_bias": scatter_about(keys[13], (2, D), 0.3, 1.75, ((0, 2), (1, 16))),
        "w_inner": scatter_about(keys[14], (2, D, FF), D ** -0.5, 0.25, ((0, 2), (1, 16))),
        "b_inner": scatter_about(keys[15], (2, FF), 0.5, 3.0, ((0, 2), (1, 16))),
        "w_outer": scatter_about(keys[16], (2, FF, D), FF ** -0.5, 0.078125, ((0, 2), (1, 16))),
        "b_outer": scatter_about(keys[17], (2, D), 0.5, 3.0, ((0, 2), (1, 16))),
    }


NORM_EPSILON = 1e-05
NEGATIVE_FILL = -1e+30

@jax.custom_vjp
def low(v):
    return lax.optimization_barrier(v.astype(jnp.bfloat16)).astype(jnp.float32)

@jax.custom_vjp
def low_back(v):
    return v

def low_keep(v):
    return (low(v), None)

def low_pass(kept, grad):
    return (grad,)

def back_keep(v):
    return (v, None)

def back_low(kept, grad):
    return (low(grad),)
low.defvjp(low_keep, low_pass)
low_back.defvjp(back_keep, back_low)

def matmul_full(left_side, right_side):
    return jnp.dot(left_side, right_side, precision=lax.Precision.HIGHEST)

def layer_norm(values, norm_gain, norm_offset):
    centred = values - lax.optimization_barrier(jnp.mean(values, axis=-1, keepdims=True))
    variance = lax.optimization_barrier(jnp.mean(centred * centred, axis=-1, keepdims=True))
    return centred * lax.rsqrt(variance + NORM_EPSILON) * norm_gain + norm_offset

def encoder_layer(hidden, valid_mask, params):
    gain_one, offset_one, query_weight, query_bias, key_weight, value_weight, value_bias, out_weight, out_bias, gain_two, offset_two, inner_weight, inner_bias, outer_weight, outer_bias = params
    length = hidden.shape[0]
    normed = low(layer_norm(hidden, gain_one, offset_one))
    queries = low_back(low(matmul_full(normed, query_weight) + query_bias)).reshape(length, HEADS, HEAD_DIM)
    keys_proj = low_back(low(matmul_full(normed, key_weight))).reshape(length, HEADS, HEAD_DIM)
    values_proj = low_back(low(matmul_full(normed, value_weight) + value_bias)).reshape(length, HEADS, HEAD_DIM)
    scores = jnp.einsum('qhd,khd->hqk', queries, keys_proj, precision=lax.Precision.HIGHEST) * (1.0 / math.sqrt(HEAD_DIM))
    scores = low_back(scores)
    scores = jnp.where(valid_mask[None, None, :] > 0.5, scores, NEGATIVE_FILL)
    attention_low = low(jax.nn.softmax(scores, axis=-1))
    mixed_heads = jnp.einsum('hqk,khd->qhd', attention_low, values_proj, precision=lax.Precision.HIGHEST).reshape(length, D)
    mixed_heads = low_back(low(mixed_heads))
    residual = hidden + low_back(matmul_full(mixed_heads, out_weight) + out_bias)
    normed_two = low(layer_norm(residual, gain_two, offset_two))
    before = low_back(matmul_full(normed_two, inner_weight) + inner_bias)
    activated = low(jax.nn.gelu(before, approximate=False))
    return (residual + low_back(matmul_full(activated, outer_weight) + outer_bias)) * valid_mask[:, None]

def reference(inputs, lengths, cotangent, ln1_gain, ln1_bias, w_query, b_query, w_key, w_value, b_value, w_out, b_out, ln2_gain, ln2_bias, w_inner, b_inner, w_outer, b_outer):
    stacked = tuple((member.astype(jnp.float32) for member in (ln1_gain, ln1_bias, w_query, b_query, w_key, w_value, b_value, w_out, b_out, ln2_gain, ln2_bias, w_inner, b_inner, w_outer, b_outer)))
    first_layer = tuple((member[0] for member in stacked))
    second_layer = tuple((member[1] for member in stacked))
    positions = jnp.arange(LEN, dtype=jnp.int32)

    def per_sequence(totals, pieces):
        sequence, seq_length, upstream = pieces
        valid_mask = (positions < seq_length).astype(jnp.float32)

        def both_layers(hidden, params_one, params_two, middle_probe):
            middle_out = encoder_layer(hidden, valid_mask, params_one)
            carried = low_back(low(middle_out) + middle_probe)
            return (middle_out, encoder_layer(carried, valid_mask, params_two))
        probe_zero = jnp.zeros((LEN, D), jnp.float32)
        (middle_out, final_out), pull_back = jax.vjp(both_layers, sequence, first_layer, second_layer, probe_zero)
        d_input, d_first, d_second, d_middle = pull_back((jnp.zeros_like(middle_out), upstream))
        totals = (jax.tree.map(jnp.add, totals[0], d_first), jax.tree.map(jnp.add, totals[1], d_second))
        return (totals, (middle_out.astype(jnp.bfloat16), final_out.astype(jnp.bfloat16), d_input.astype(jnp.bfloat16), d_middle.astype(jnp.bfloat16)))
    start_totals = (jax.tree.map(jnp.zeros_like, first_layer), jax.tree.map(jnp.zeros_like, second_layer))
    totals, stacked_out = lax.scan(per_sequence, start_totals, (inputs.astype(jnp.float32), lengths, cotangent.astype(jnp.float32)))
    middles, finals, d_inputs, d_middles = stacked_out
    layer_out = jnp.stack([middles, finals])
    input_grads = jnp.stack([d_inputs, d_middles])
    grads = tuple((jnp.stack([one_member, two_member]) for one_member, two_member in zip(totals[0], totals[1])))
    return (layer_out, input_grads, grads[0], grads[1], grads[2], grads[3], grads[4], grads[5], grads[6], grads[7], grads[8], grads[9], grads[10], grads[11], grads[12], grads[13], grads[14])
```

```python
import math

import jax
import jax.numpy as jnp
from jax import lax
from jax.sharding import Mesh, PartitionSpec as P

HEADS = 20
HEAD_DIM = 32
NORM_EPSILON = 1e-05
NEGATIVE_FILL = -1e30
SCALE = 1.0 / math.sqrt(HEAD_DIM)
BF = jnp.bfloat16
F32 = jnp.float32


def swap(a, axis):
    return lax.ppermute(a, axis, [(0, 1), (1, 0)])


def send(a, axis, source):
    return lax.ppermute(a, axis, [(source, 1 - source)])


def dot(a, b):
    return jnp.dot(a, b, preferred_element_type=F32)


def dot_t(a, b):
    return lax.dot_general(a, b, (((1,), (1,)), ((), ())), preferred_element_type=F32)


def dot_o(a, b):
    return lax.dot_general(a, b, (((0,), (0,)), ((), ())), preferred_element_type=F32)


def pair(mine, other, index):
    return jnp.stack([jnp.where(index == 0, mine, other), jnp.where(index == 0, other, mine)])


def pick(a, index):
    return lax.dynamic_index_in_dim(a, index, 0, keepdims=False)


def gather_chips(piece, z, x):
    count = lax.axis_size("z")
    if count > 4:
        columns = lax.all_gather(piece, "z", axis=0)
        other = swap(columns, "x")
        return jnp.moveaxis(pair(columns, other, x), 0, 1)
    own = [piece]
    other = [swap(piece, "x")]
    for k in range(1, count):
        moved = lax.ppermute(piece, "z", [((i + k) % count, i) for i in range(count)])
        own.append(moved)
        other.append(swap(moved, "x"))
    both = jnp.moveaxis(pair(jnp.stack(own), jnp.stack(other), x), 0, 1)
    twice = jnp.concatenate([both, both], axis=0)
    return lax.dynamic_slice_in_dim(twice, count - z, count, axis=0)


def reduce_chips(parts, z, x):
    count = lax.axis_size("z")
    split = jnp.moveaxis(parts, 1, 0)
    moved = swap(pick(split, 1 - x), "x")
    column = (pick(split, x).astype(F32) + moved.astype(F32)).astype(BF)
    if count > 4:
        return lax.psum_scatter(column.astype(F32), "z", scatter_dimension=0, tiled=False)
    total = pick(column, z).astype(F32)
    for k in range(1, count):
        block = pick(column, lax.rem(z + k, count))
        total = total + lax.ppermute(block, "z", [(i, (i + k) % count) for i in range(count)]).astype(F32)
    return total


def layer_norm(values):
    centred = values - jnp.mean(values, axis=-1, keepdims=True)
    variance = jnp.mean(centred * centred, axis=-1, keepdims=True)
    inverse = lax.rsqrt(variance + NORM_EPSILON)
    return centred * inverse, inverse


def norm_back(upstream, unit, inverse, gain):
    scaled = upstream * gain
    return inverse * (
        scaled
        - jnp.mean(scaled, axis=-1, keepdims=True)
        - unit * jnp.mean(scaled * unit, axis=-1, keepdims=True)
    )


def split_heads(a, seqs):
    return a.reshape(seqs, a.shape[0] // seqs, HEADS, HEAD_DIM)


def probabilities(q, k, keys_valid):
    scores = jnp.einsum("sqhd,skhd->shqk", q, k, preferred_element_type=F32) * SCALE
    scores = jnp.where(keys_valid[:, None, None, :] > 0.5, scores, NEGATIVE_FILL)
    shifted = jnp.exp(scores - jnp.max(scores, axis=-1, keepdims=True))
    return shifted / jnp.sum(shifted, axis=-1, keepdims=True)


def attention_forward(rows, keys_valid, weights, vectors):
    wq, wk, wv, wo = weights
    seqs = keys_valid.shape[0]
    hidden = rows.astype(F32)
    unit, _ = layer_norm(hidden)
    normed = (unit * vectors[0] + vectors[1]).astype(BF)
    q = (dot(normed, wq) + vectors[2]).astype(BF)
    k = dot(normed, wk).astype(BF)
    v = (dot(normed, wv) + vectors[3]).astype(BF)
    probs = probabilities(split_heads(q, seqs), split_heads(k, seqs), keys_valid).astype(BF)
    mixed = (
        jnp.einsum("shqk,skhd->sqhd", probs, split_heads(v, seqs), preferred_element_type=F32)
        .reshape(rows.shape)
        .astype(BF)
    )
    residual = hidden + dot(mixed, wo) + vectors[4]
    unit_two, _ = layer_norm(residual)
    normed_two = (unit_two * vectors[5] + vectors[6]).astype(BF)
    return residual, normed_two, (rows, q, k, v, mixed, residual)


def attention_backward(saved, d_out, d_normed_two, keys_valid, weights, vectors):
    rows, q, k, v, mixed, residual = saved
    wq, wk, wv, wo = weights
    seqs = keys_valid.shape[0]
    unit_two, inverse_two = layer_norm(residual)
    d_residual = d_out + norm_back(d_normed_two, unit_two, inverse_two, vectors[5])
    d_attn = d_residual.astype(BF)
    d_mixed = dot_t(d_attn, wo).astype(BF)
    g_out = dot_o(mixed, d_attn)
    qh, kh, vh, dh = (split_heads(a, seqs) for a in (q, k, v, d_mixed))
    probs = probabilities(qh, kh, keys_valid)
    d_values = jnp.einsum("shqk,sqhd->skhd", probs.astype(BF), dh, preferred_element_type=F32)
    d_probs = jnp.einsum("sqhd,skhd->shqk", dh, vh, preferred_element_type=F32)
    d_scores = (probs * (d_probs - jnp.sum(probs * d_probs, axis=-1, keepdims=True))).astype(BF)
    d_queries = jnp.einsum("shqk,skhd->sqhd", d_scores, kh, preferred_element_type=F32) * SCALE
    d_keys = jnp.einsum("shqk,sqhd->skhd", d_scores, qh, preferred_element_type=F32) * SCALE
    dq, dk, dv = (a.reshape(rows.shape).astype(BF) for a in (d_queries, d_keys, d_values))
    unit, inverse = layer_norm(rows.astype(F32))
    normed = (unit * vectors[0] + vectors[1]).astype(BF)
    d_normed = dot_t(dq, wq) + dot_t(dk, wk) + dot_t(dv, wv)
    d_input = d_residual + norm_back(d_normed, unit, inverse, vectors[0])
    matrices = jnp.stack([dot_o(normed, dq), dot_o(normed, dk), dot_o(normed, dv), g_out]).astype(BF)

    def total(a):
        return jnp.sum(a.astype(F32), axis=0)

    sums = jnp.stack(
        [
            total(d_normed * unit),
            total(d_normed),
            total(dq),
            total(dv),
            total(d_attn),
            total(d_normed_two * unit_two),
            total(d_normed_two),
            total(d_out.astype(BF)),
        ]
    )
    return d_input.astype(BF), matrices, sums


def ff_forward(normed_two, inner, bias, outer):
    before = dot(normed_two, inner) + bias
    normal = 0.5 * (1.0 + lax.erf(before * (1.0 / math.sqrt(2.0))))
    slope = normal + before * jnp.exp(-0.5 * before * before) * (1.0 / math.sqrt(2.0 * math.pi))
    activated = (before * normal).astype(BF)
    return dot(activated, outer), activated, slope


def ff_backward(normed_two, activated, slope, branch, inner, outer):
    d_before = (dot_t(branch, outer) * slope).astype(BF)
    d_normed_two = dot_t(d_before, inner)
    g_outer = dot_o(activated, branch).astype(BF)
    g_inner = dot_o(normed_two, d_before).astype(BF)
    g_bias = jnp.sum(d_before.astype(F32), axis=0).astype(BF)
    return d_normed_two, g_inner, g_bias, g_outer


def per_device(inputs, lengths, cotangent, *params):
    (
        ln1_gain,
        ln1_bias,
        w_query,
        b_query,
        w_key,
        w_value,
        b_value,
        w_out,
        b_out,
        ln2_gain,
        ln2_bias,
        w_inner,
        b_inner,
        w_outer,
        b_outer,
    ) = (a[0] for a in params)
    y, z, x, c = (lax.axis_index(name) for name in ("section", "z", "x", "core"))
    chips = lax.axis_size("z") * 2
    seqs, length, width = inputs.shape
    tokens = seqs * length
    rows = w_query.shape[0]
    units = w_outer.shape[0]
    half = units // 2
    hidden = chips * half
    valid = (jnp.arange(length, dtype=jnp.int32)[None, :] < lengths[:, None]).astype(F32)
    row_valid = valid.reshape(tokens, 1)

    small = jnp.stack([ln1_gain, ln1_bias, b_query, b_value, b_out, ln2_gain, ln2_bias, b_outer])
    small = jnp.pad(small.reshape(1, 8 * rows), ((0, 7), (0, width - 8 * rows)))
    attention_piece = jnp.concatenate([w_query, w_key, w_value, w_out, small])
    gathered = gather_chips(attention_piece, z, x)
    gathered = jnp.moveaxis(pair(gathered, swap(gathered, "core"), c), 0, 2)
    weights = tuple(
        gathered[:, :, :, k * rows : (k + 1) * rows].reshape(width, width) for k in range(4)
    )
    vectors = gathered[:, :, :, 4 * rows, : 8 * rows].reshape(chips * 2, 8, rows)
    vectors = jnp.moveaxis(vectors, 1, 0).reshape(8, width).astype(F32)

    outer_halves = jnp.pad(
        jnp.concatenate(
            [
                w_outer.reshape(2, half, width),
                jnp.pad(b_inner.reshape(2, 1, half), ((0, 0), (0, 0), (0, width - half))),
            ],
            axis=1,
        ),
        ((0, 0), (0, 7), (0, 0)),
    )
    outer_both = pair(pick(outer_halves, y), swap(pick(outer_halves, 1 - y), "section"), y)
    quarters = w_inner.reshape(rows, chips, 2, 2, half).transpose(3, 2, 0, 1, 4).reshape(2, 2, rows, hidden)
    inner_both = pair(pick(quarters, y), swap(pick(quarters, 1 - y), "section"), y)
    inner, outer, bias = [], [], []
    for layer in range(2):
        mine = inner_both[layer]
        piece = pair(pick(mine, c), swap(pick(mine, 1 - c), "core"), c).reshape(2 * rows, hidden)
        inner.append(gather_chips(piece, z, x).reshape(width, hidden))
        outer_all = gather_chips(outer_both[layer], z, x)
        outer.append(outer_all[:, :, :half].reshape(hidden, width))
        bias.append(outer_all[:, :, half, :half].reshape(hidden).astype(F32))

    def spread(own, source):
        if source is not None:
            own = jnp.where(y == source, own, send(own, "section", source))
        return jnp.concatenate([own, swap(own, "core")])

    def core_sum(partial):
        return partial[:tokens] + swap(partial[tokens:].astype(BF), "core").astype(F32)

    outputs, saved, ff_saved = [], [], []
    current = inputs.reshape(tokens, width)
    for layer in range(2):
        residual, normed_two, kept = attention_forward(current, valid, weights, vectors)
        saved.append(kept)
        normed_all = spread(normed_two, layer)
        partial, activated, slope = ff_forward(normed_all, inner[layer], bias[layer], outer[layer])
        ff_saved.append((normed_all, activated, slope))
        own = core_sum(partial)
        own = jnp.where(y == layer, own + residual + vectors[7], own)
        low = own.astype(BF)
        current = ((own + swap(low, "section").astype(F32)) * row_valid).astype(BF)
        outputs.append(current)
    layer_out = jnp.where(y == 0, outputs[0], outputs[1])

    inner_grads, outer_grads = [None, None], [None, None]
    attention_grads, input_grads = [None, None], [None, None]
    upstream = cotangent.reshape(tokens, width)
    for layer in (1, 0):
        branch = (upstream.astype(F32) * row_valid).astype(BF)
        branch_all = spread(branch, None if layer == 1 else 1)
        d_out = branch_all[:tokens].astype(F32)
        d_partial, g_inner, g_bias, g_outer = ff_backward(
            *ff_saved[layer], branch_all, inner[layer], outer[layer]
        )
        g_bias = jnp.pad(g_bias.reshape(chips, 1, half), ((0, 0), (0, 7), (0, width - half)))
        g_outer = jnp.concatenate([g_outer.reshape(chips, half, width), g_bias], axis=1)
        outer_grads[layer] = reduce_chips(g_outer.reshape((chips // 2, 2) + g_outer.shape[1:]), z, x)
        inner_grads[layer] = reduce_chips(g_inner.reshape(chips // 2, 2, 2 * rows, hidden), z, x)
        own = core_sum(d_partial)
        d_normed_two = own + send(own.astype(BF), "section", 1 - layer).astype(F32)
        upstream, matrices, sums = attention_backward(
            saved[layer], d_out, d_normed_two, valid, weights, vectors
        )
        input_grads[layer] = upstream
        attention_grads[layer] = (matrices, sums)
    input_grad = jnp.where(y == 0, input_grads[0], input_grads[1])

    matrices, sums = (jnp.where(y == 0, a, b) for a, b in zip(*attention_grads))
    matrices = matrices.reshape(4, chips * 2, rows, width).transpose(1, 0, 2, 3).reshape(chips * 2, 4 * rows, width)
    sums = jnp.moveaxis(sums.reshape(8, chips * 2, rows), 0, 1).reshape(chips * 2, 1, 8 * rows).astype(BF)
    sums = jnp.pad(sums, ((0, 0), (0, 7), (0, width - 8 * rows)))
    parts = jnp.concatenate([matrices, sums], axis=1).reshape(chips, 2, 4 * rows + 8, width)
    parts = jnp.moveaxis(parts, 1, 0)
    parts = (pick(parts, c).astype(F32) + swap(pick(parts, 1 - c), "core").astype(F32)).astype(BF)
    attention = reduce_chips(parts.reshape(chips // 2, 2, 4 * rows + 8, width), z, x)
    g_query, g_key, g_value, g_out = (attention[k * rows : (k + 1) * rows] for k in range(4))
    g_small = attention[4 * rows, : 8 * rows].reshape(8, rows)

    def home(pieces):
        mine = jnp.where(y == 0, pieces[0], pieces[1])
        other = jnp.where(
            y == 0,
            send(pieces[0].astype(BF), "section", 1),
            send(pieces[1].astype(BF), "section", 0),
        ).astype(F32)
        return pair(mine, other, y)

    for layer in range(2):
        halves = inner_grads[layer].reshape(2, rows, hidden)
        inner_grads[layer] = pair(
            pick(halves, c), swap(pick(halves, 1 - c).astype(BF), "core").astype(F32), c
        )
    g_inner = home(inner_grads).reshape(2, 2, rows, chips, half).transpose(2, 3, 1, 0, 4).reshape(rows, 2 * units * chips)
    outer_home = home(outer_grads)
    g_outer = outer_home[:, :half].reshape(units, width)
    g_bias = outer_home[:, half, :half].reshape(units)
    return (
        layer_out.reshape(1, seqs, length, width),
        input_grad.reshape(1, seqs, length, width),
        g_small[0:1],
        g_small[1:2],
        g_query[None],
        g_small[2:3],
        g_key[None],
        g_value[None],
        g_small[3:4],
        g_out[None],
        g_small[4:5],
        g_small[5:6],
        g_small[6:7],
        g_inner[None],
        g_bias[None],
        g_outer[None],
        g_small[7:8],
    )


def solution(mesh):
    sections, dp = mesh.devices.shape
    fine = Mesh(mesh.devices.reshape(sections, dp // 4, 2, 2), ("section", "z", "x", "core"))
    rows = ("z", "x", "core")
    vector, matrix = P("section", rows), P("section", rows, None)
    stacked = P("section", rows, None, None)
    kinds = (
        vector, vector, matrix, vector, matrix, matrix, vector, matrix,
        vector, vector, vector, matrix, vector, matrix, vector,
    )
    return jax.shard_map(
        per_device,
        mesh=fine,
        in_specs=(P(rows, None, None), P(rows), P(rows, None, None)) + kinds,
        out_specs=(stacked, stacked) + kinds,
        check_vma=False,
    )
```

```python
import math

import jax
import jax.numpy as jnp
from jax import lax
from jax.experimental import pallas as pl
from jax.experimental.pallas import tpu as pltpu
from jax.sharding import Mesh, PartitionSpec as P

HEADS = 20
HEAD_DIM = 32
NORM_EPSILON = 1e-05
NEGATIVE_FILL = -1e30
SCALE = 1.0 / math.sqrt(HEAD_DIM)
BF = jnp.bfloat16
F32 = jnp.float32


def swap(a, axis):
    return lax.ppermute(a, axis, [(0, 1), (1, 0)])


def send(a, axis, source):
    return lax.ppermute(a, axis, [(source, 1 - source)])


def dot(a, b):
    return jnp.dot(a, b, preferred_element_type=F32)


def dot_t(a, b):
    return lax.dot_general(a, b, (((1,), (1,)), ((), ())), preferred_element_type=F32)


def dot_o(a, b):
    return lax.dot_general(a, b, (((0,), (0,)), ((), ())), preferred_element_type=F32)


def pair(mine, other, index):
    return jnp.stack([jnp.where(index == 0, mine, other), jnp.where(index == 0, other, mine)])


def pick(a, index):
    return lax.dynamic_index_in_dim(a, index, 0, keepdims=False)


def gather_chips(piece, z, x):
    count = lax.axis_size("z")
    if count > 4:
        columns = lax.all_gather(piece, "z", axis=0)
        other = swap(columns, "x")
        return jnp.moveaxis(pair(columns, other, x), 0, 1)
    own = [piece]
    other = [swap(piece, "x")]
    for k in range(1, count):
        moved = lax.ppermute(piece, "z", [((i + k) % count, i) for i in range(count)])
        own.append(moved)
        other.append(swap(moved, "x"))
    both = jnp.moveaxis(pair(jnp.stack(own), jnp.stack(other), x), 0, 1)
    twice = jnp.concatenate([both, both], axis=0)
    return lax.dynamic_slice_in_dim(twice, count - z, count, axis=0)


def reduce_chips(parts, z, x):
    count = lax.axis_size("z")
    split = jnp.moveaxis(parts, 1, 0)
    moved = swap(pick(split, 1 - x), "x")
    column = (pick(split, x).astype(F32) + moved.astype(F32)).astype(BF)
    if count > 4:
        return lax.psum_scatter(column.astype(F32), "z", scatter_dimension=0, tiled=False)
    total = pick(column, z).astype(F32)
    for k in range(1, count):
        block = pick(column, lax.rem(z + k, count))
        total = total + lax.ppermute(block, "z", [(i, (i + k) % count) for i in range(count)]).astype(F32)
    return total


def layer_norm(values):
    centred = values - jnp.mean(values, axis=-1, keepdims=True)
    variance = jnp.mean(centred * centred, axis=-1, keepdims=True)
    inverse = lax.rsqrt(variance + NORM_EPSILON)
    return centred * inverse, inverse


def norm_back(upstream, unit, inverse, gain):
    scaled = upstream * gain
    return inverse * (
        scaled
        - jnp.mean(scaled, axis=-1, keepdims=True)
        - unit * jnp.mean(scaled * unit, axis=-1, keepdims=True)
    )


def split_heads(a, seqs):
    return a.reshape(seqs, a.shape[0] // seqs, HEADS, HEAD_DIM)


def probabilities(q, k, keys_valid):
    scores = jnp.einsum("sqhd,skhd->shqk", q, k, preferred_element_type=F32) * SCALE
    scores = jnp.where(keys_valid[:, None, None, :] > 0.5, scores, NEGATIVE_FILL)
    shifted = jnp.exp(scores - jnp.max(scores, axis=-1, keepdims=True))
    return shifted / jnp.sum(shifted, axis=-1, keepdims=True)


def attention_forward(rows, keys_valid, weights, vectors):
    wq, wk, wv, wo = weights
    seqs = keys_valid.shape[0]
    hidden = rows.astype(F32)
    unit, _ = layer_norm(hidden)
    normed = (unit * vectors[0] + vectors[1]).astype(BF)
    q = (dot(normed, wq) + vectors[2]).astype(BF)
    k = dot(normed, wk).astype(BF)
    v = (dot(normed, wv) + vectors[3]).astype(BF)
    probs = probabilities(split_heads(q, seqs), split_heads(k, seqs), keys_valid).astype(BF)
    mixed = (
        jnp.einsum("shqk,skhd->sqhd", probs, split_heads(v, seqs), preferred_element_type=F32)
        .reshape(rows.shape)
        .astype(BF)
    )
    residual = hidden + dot(mixed, wo) + vectors[4]
    unit_two, _ = layer_norm(residual)
    normed_two = (unit_two * vectors[5] + vectors[6]).astype(BF)
    return residual, normed_two, (rows, q, k, v, mixed, residual)


def attention_backward(saved, d_out, d_normed_two, keys_valid, weights, vectors):
    rows, q, k, v, mixed, residual = saved
    wq, wk, wv, wo = weights
    seqs = keys_valid.shape[0]
    unit_two, inverse_two = layer_norm(residual)
    d_residual = d_out + norm_back(d_normed_two, unit_two, inverse_two, vectors[5])
    d_attn = d_residual.astype(BF)
    d_mixed = dot_t(d_attn, wo).astype(BF)
    g_out = dot_o(mixed, d_attn)
    qh, kh, vh, dh = (split_heads(a, seqs) for a in (q, k, v, d_mixed))
    probs = probabilities(qh, kh, keys_valid)
    d_values = jnp.einsum("shqk,sqhd->skhd", probs.astype(BF), dh, preferred_element_type=F32)
    d_probs = jnp.einsum("sqhd,skhd->shqk", dh, vh, preferred_element_type=F32)
    d_scores = (probs * (d_probs - jnp.sum(probs * d_probs, axis=-1, keepdims=True))).astype(BF)
    d_queries = jnp.einsum("shqk,skhd->sqhd", d_scores, kh, preferred_element_type=F32) * SCALE
    d_keys = jnp.einsum("shqk,sqhd->skhd", d_scores, qh, preferred_element_type=F32) * SCALE
    dq, dk, dv = (a.reshape(rows.shape).astype(BF) for a in (d_queries, d_keys, d_values))
    unit, inverse = layer_norm(rows.astype(F32))
    normed = (unit * vectors[0] + vectors[1]).astype(BF)
    d_normed = dot_t(dq, wq) + dot_t(dk, wk) + dot_t(dv, wv)
    d_input = d_residual + norm_back(d_normed, unit, inverse, vectors[0])
    matrices = jnp.stack([dot_o(normed, dq), dot_o(normed, dk), dot_o(normed, dv), g_out]).astype(BF)

    def total(a):
        return jnp.sum(a.astype(F32), axis=0)

    sums = jnp.stack(
        [
            total(d_normed * unit),
            total(d_normed),
            total(dq),
            total(dv),
            total(d_attn),
            total(d_normed_two * unit_two),
            total(d_normed_two),
            total(d_out.astype(BF)),
        ]
    )
    return d_input.astype(BF), matrices, sums


def ff_forward(normed_two, inner, bias, outer):
    before = dot(normed_two, inner) + bias
    normal = 0.5 * (1.0 + lax.erf(before * (1.0 / math.sqrt(2.0))))
    slope = normal + before * jnp.exp(-0.5 * before * before) * (1.0 / math.sqrt(2.0 * math.pi))
    activated = (before * normal).astype(BF)
    return dot(activated, outer), activated, slope


def ff_backward(normed_two, activated, slope, branch, inner, outer):
    d_before = (dot_t(branch, outer) * slope).astype(BF)
    d_normed_two = dot_t(d_before, inner)
    g_outer = dot_o(activated, branch).astype(BF)
    g_inner = dot_o(normed_two, d_before).astype(BF)
    g_bias = jnp.sum(d_before.astype(F32), axis=0).astype(BF)
    return d_normed_two, g_inner, g_bias, g_outer


def per_device_general(inputs, lengths, cotangent, *params):
    (
        ln1_gain,
        ln1_bias,
        w_query,
        b_query,
        w_key,
        w_value,
        b_value,
        w_out,
        b_out,
        ln2_gain,
        ln2_bias,
        w_inner,
        b_inner,
        w_outer,
        b_outer,
    ) = (a[0] for a in params)
    y, z, x, c = (lax.axis_index(name) for name in ("section", "z", "x", "core"))
    chips = lax.axis_size("z") * 2
    seqs, length, width = inputs.shape
    tokens = seqs * length
    rows = w_query.shape[0]
    units = w_outer.shape[0]
    half = units // 2
    hidden = chips * half
    valid = (jnp.arange(length, dtype=jnp.int32)[None, :] < lengths[:, None]).astype(F32)
    row_valid = valid.reshape(tokens, 1)

    small = jnp.stack([ln1_gain, ln1_bias, b_query, b_value, b_out, ln2_gain, ln2_bias, b_outer])
    small = jnp.pad(small.reshape(1, 8 * rows), ((0, 7), (0, width - 8 * rows)))
    attention_piece = jnp.concatenate([w_query, w_key, w_value, w_out, small])
    gathered = gather_chips(attention_piece, z, x)
    gathered = jnp.moveaxis(pair(gathered, swap(gathered, "core"), c), 0, 2)
    weights = tuple(
        gathered[:, :, :, k * rows : (k + 1) * rows].reshape(width, width) for k in range(4)
    )
    vectors = gathered[:, :, :, 4 * rows, : 8 * rows].reshape(chips * 2, 8, rows)
    vectors = jnp.moveaxis(vectors, 1, 0).reshape(8, width).astype(F32)

    outer_halves = jnp.pad(
        jnp.concatenate(
            [
                w_outer.reshape(2, half, width),
                jnp.pad(b_inner.reshape(2, 1, half), ((0, 0), (0, 0), (0, width - half))),
            ],
            axis=1,
        ),
        ((0, 0), (0, 7), (0, 0)),
    )
    outer_both = pair(pick(outer_halves, y), swap(pick(outer_halves, 1 - y), "section"), y)
    quarters = w_inner.reshape(rows, chips, 2, 2, half).transpose(3, 2, 0, 1, 4).reshape(2, 2, rows, hidden)
    inner_both = pair(pick(quarters, y), swap(pick(quarters, 1 - y), "section"), y)
    inner, outer, bias = [], [], []
    for layer in range(2):
        mine = inner_both[layer]
        piece = pair(pick(mine, c), swap(pick(mine, 1 - c), "core"), c).reshape(2 * rows, hidden)
        inner.append(gather_chips(piece, z, x).reshape(width, hidden))
        outer_all = gather_chips(outer_both[layer], z, x)
        outer.append(outer_all[:, :, :half].reshape(hidden, width))
        bias.append(outer_all[:, :, half, :half].reshape(hidden).astype(F32))

    def spread(own, source):
        if source is not None:
            own = jnp.where(y == source, own, send(own, "section", source))
        return jnp.concatenate([own, swap(own, "core")])

    def core_sum(partial):
        return partial[:tokens] + swap(partial[tokens:].astype(BF), "core").astype(F32)

    outputs, saved, ff_saved = [], [], []
    current = inputs.reshape(tokens, width)
    for layer in range(2):
        residual, normed_two, kept = attention_forward(current, valid, weights, vectors)
        saved.append(kept)
        normed_all = spread(normed_two, layer)
        partial, activated, slope = ff_forward(normed_all, inner[layer], bias[layer], outer[layer])
        ff_saved.append((normed_all, activated, slope))
        own = core_sum(partial)
        own = jnp.where(y == layer, own + residual + vectors[7], own)
        low = own.astype(BF)
        current = ((own + swap(low, "section").astype(F32)) * row_valid).astype(BF)
        outputs.append(current)
    layer_out = jnp.where(y == 0, outputs[0], outputs[1])

    inner_grads, outer_grads = [None, None], [None, None]
    attention_grads, input_grads = [None, None], [None, None]
    upstream = cotangent.reshape(tokens, width)
    for layer in (1, 0):
        branch = (upstream.astype(F32) * row_valid).astype(BF)
        branch_all = spread(branch, None if layer == 1 else 1)
        d_out = branch_all[:tokens].astype(F32)
        d_partial, g_inner, g_bias, g_outer = ff_backward(
            *ff_saved[layer], branch_all, inner[layer], outer[layer]
        )
        g_bias = jnp.pad(g_bias.reshape(chips, 1, half), ((0, 0), (0, 7), (0, width - half)))
        g_outer = jnp.concatenate([g_outer.reshape(chips, half, width), g_bias], axis=1)
        outer_grads[layer] = reduce_chips(g_outer.reshape((chips // 2, 2) + g_outer.shape[1:]), z, x)
        inner_grads[layer] = reduce_chips(g_inner.reshape(chips // 2, 2, 2 * rows, hidden), z, x)
        own = core_sum(d_partial)
        d_normed_two = own + send(own.astype(BF), "section", 1 - layer).astype(F32)
        upstream, matrices, sums = attention_backward(
            saved[layer], d_out, d_normed_two, valid, weights, vectors
        )
        input_grads[layer] = upstream
        attention_grads[layer] = (matrices, sums)
    input_grad = jnp.where(y == 0, input_grads[0], input_grads[1])

    matrices, sums = (jnp.where(y == 0, a, b) for a, b in zip(*attention_grads))
    matrices = matrices.reshape(4, chips * 2, rows, width).transpose(1, 0, 2, 3).reshape(chips * 2, 4 * rows, width)
    sums = jnp.moveaxis(sums.reshape(8, chips * 2, rows), 0, 1).reshape(chips * 2, 1, 8 * rows).astype(BF)
    sums = jnp.pad(sums, ((0, 0), (0, 7), (0, width - 8 * rows)))
    parts = jnp.concatenate([matrices, sums], axis=1).reshape(chips, 2, 4 * rows + 8, width)
    parts = jnp.moveaxis(parts, 1, 0)
    parts = (pick(parts, c).astype(F32) + swap(pick(parts, 1 - c), "core").astype(F32)).astype(BF)
    attention = reduce_chips(parts.reshape(chips // 2, 2, 4 * rows + 8, width), z, x)
    g_query, g_key, g_value, g_out = (attention[k * rows : (k + 1) * rows] for k in range(4))
    g_small = attention[4 * rows, : 8 * rows].reshape(8, rows)

    def home(pieces):
        mine = jnp.where(y == 0, pieces[0], pieces[1])
        other = jnp.where(
            y == 0,
            send(pieces[0].astype(BF), "section", 1),
            send(pieces[1].astype(BF), "section", 0),
        ).astype(F32)
        return pair(mine, other, y)

    for layer in range(2):
        halves = inner_grads[layer].reshape(2, rows, hidden)
        inner_grads[layer] = pair(
            pick(halves, c), swap(pick(halves, 1 - c).astype(BF), "core").astype(F32), c
        )
    g_inner = home(inner_grads).reshape(2, 2, rows, chips, half).transpose(2, 3, 1, 0, 4).reshape(rows, 2 * units * chips)
    outer_home = home(outer_grads)
    g_outer = outer_home[:, :half].reshape(units, width)
    g_bias = outer_home[:, half, :half].reshape(units)
    return (
        layer_out.reshape(1, seqs, length, width),
        input_grad.reshape(1, seqs, length, width),
        g_small[0:1],
        g_small[1:2],
        g_query[None],
        g_small[2:3],
        g_key[None],
        g_value[None],
        g_small[3:4],
        g_out[None],
        g_small[4:5],
        g_small[5:6],
        g_small[6:7],
        g_inner[None],
        g_bias[None],
        g_outer[None],
        g_small[7:8],
    )


def whole(shape):
    return pl.BlockSpec(shape, lambda *_: (0,) * len(shape))


ANY = pl.BlockSpec(memory_space=pl.ANY)


def call(body, order, arrays, specs, shapes, scratch=(), flops=0, name=None):
    shapes = [jax.ShapeDtypeStruct(s, d) for s, d in shapes]
    moved = sum(a.size * a.dtype.itemsize for a in list(arrays) + shapes)
    return pl.pallas_call(
        body,
        out_shape=shapes,
        grid_spec=pltpu.PrefetchScalarGridSpec(
            num_scalar_prefetch=1,
            grid=(1,),
            in_specs=specs,
            out_specs=[whole(s.shape) for s in shapes],
            scratch_shapes=list(scratch),
        ),
        compiler_params=pltpu.CompilerParams(vmem_limit_bytes=56 * 1024 * 1024),
        cost_estimate=pl.CostEstimate(flops=flops, bytes_accessed=moved, transcendentals=0),
        name=name,
    )(order, *arrays)


def run_copies(copies):
    for copy in copies:
        copy.start()
    for copy in copies:
        copy.wait()


def join_attention(order, own, received):
    slots = len(own)
    height, width = own[0].shape
    rows = (height - 8) // 4

    def body(order_ref, *refs):
        own_refs, received_ref = refs[:slots], refs[slots]
        matrices, vectors, small, sems = refs[slots + 1 :]
        copies = []
        for i in range(2 * slots):
            piece = own_refs[i] if i < slots else received_ref.at[i - slots]
            owner = order_ref[i]
            start = pl.multiple_of(owner * rows, 8)
            for k in range(4):
                copies.append(
                    pltpu.make_async_copy(
                        piece.at[pl.ds(k * rows, rows), :],
                        matrices.at[k, pl.ds(start, rows), :],
                        sems.at[i, k],
                    )
                )
            copies.append(
                pltpu.make_async_copy(piece.at[pl.ds(4 * rows, 8), :], small.at[owner], sems.at[i, 4])
            )
        run_copies(copies)
        total = small[0].astype(F32)
        for i in range(1, 2 * slots):
            total = total + pltpu.roll(small[i].astype(F32), i * rows, 1)
        vectors[...] = total

    return call(
        body,
        order,
        list(own) + [received],
        [ANY] * (slots + 1),
        [((4, width, width), BF), ((8, width), F32)],
        [pltpu.VMEM((2 * slots, 8, width), BF), pltpu.SemaphoreType.DMA((2 * slots, 5))],
        name="join_attention",
    )


def head_masks(dtype):
    lane = lax.broadcasted_iota(jnp.int32, (1, 128), 1) // HEAD_DIM
    return [(lane == h).astype(F32).astype(dtype) for h in range(128 // HEAD_DIM)]


def stacked(a, masks):
    return jnp.concatenate([a * m for m in masks], axis=0)


def beside(a):
    return jnp.concatenate([a[i * 128 : (i + 1) * 128] for i in range(a.shape[0] // 128)], axis=1)


def kernel_probabilities(q_stack, k, keys):
    scores = dot_t(q_stack, k) * SCALE
    scores = jnp.where(keys > 0.5, scores, NEGATIVE_FILL)
    shifted = jnp.exp(scores - jnp.max(scores, axis=-1, keepdims=True))
    return shifted / jnp.sum(shifted, axis=-1, keepdims=True)


def windows(index, groups):
    s, g = index // groups, lax.rem(index, groups)
    return s, pl.ds(pl.multiple_of(s * 128, 128), 128), pl.ds(pl.multiple_of(g * 128, 128), 128)


def attention_forward_kernel(order, rows, valid, matrices, vectors):
    tokens, width = rows.shape
    seqs = valid.shape[0]
    groups = width // 128

    def body(order_ref, rows_ref, valid_ref, w_ref, vec_ref, res_ref, n2_ref, q_ref, k_ref, v_ref, mix_ref):
        hidden = rows_ref[...].astype(F32)
        unit, _ = layer_norm(hidden)
        normed = (unit * vec_ref[0:1] + vec_ref[1:2]).astype(BF)
        q_ref[...] = (dot(normed, w_ref[0]) + vec_ref[2:3]).astype(BF)
        k_ref[...] = dot(normed, w_ref[1]).astype(BF)
        v_ref[...] = (dot(normed, w_ref[2]) + vec_ref[3:4]).astype(BF)
        masks = head_masks(BF)

        def group(index, _):
            s, r, l = windows(index, groups)
            probs = kernel_probabilities(stacked(q_ref[r, l], masks), k_ref[r, l], valid_ref[pl.ds(s, 1)])
            mix_ref[r, l] = dot(beside(probs.astype(BF)), stacked(v_ref[r, l], masks)).astype(BF)
            return 0

        lax.fori_loop(0, seqs * groups, group, 0)
        residual = rows_ref[...].astype(F32) + dot(mix_ref[...], w_ref[3]) + vec_ref[4:5]
        res_ref[...] = residual
        unit_two, _ = layer_norm(residual)
        n2_ref[...] = (unit_two * vec_ref[5:6] + vec_ref[6:7]).astype(BF)

    low = ((tokens, width), BF)
    return call(
        body,
        order,
        [rows, valid, matrices, vectors],
        [whole(a.shape) for a in (rows, valid, matrices, vectors)],
        [((tokens, width), F32)] + [low] * 5,
        flops=8 * tokens * width * width,
        name="attention_forward",
    )


def attention_backward_kernel(order, branch, dn_own, dn_other, saved, valid, matrices, vectors, slots):
    rows, q, k, v, mixed, residual = saved
    tokens, width = rows.shape
    seqs = valid.shape[0]
    groups = width // 128
    part = width // (2 * slots)

    def body(
        order_ref, branch_ref, own_ref, other_ref, rows_ref, q_ref, k_ref, v_ref, mix_ref, res_ref,
        valid_ref, w_ref, vec_ref, dx_ref, g_ref, dm_ref, dq_ref, dk_ref, dv_ref, dr_ref,
    ):
        core = order_ref[0]

        def put(block, low, height):
            for i in range(2 * slots):
                place = jnp.bitwise_xor(core, i % 2)
                g_ref[place, order_ref[1 + i // 2], pl.ds(low, height), :] = block(i)

        d_out = branch_ref[...].astype(F32)
        d_n2 = own_ref[...] + other_ref[...].astype(F32)
        unit_two, inverse_two = layer_norm(res_ref[...])
        d_residual = d_out + norm_back(d_n2, unit_two, inverse_two, vec_ref[5:6])
        dr_ref[...] = d_residual
        d_attn = d_residual.astype(BF)
        sums = [jnp.sum(d_attn.astype(F32), axis=0, keepdims=True)]
        sums += [jnp.sum(a, axis=0, keepdims=True) for a in (d_n2 * unit_two, d_n2, d_out)]
        dm_ref[...] = dot_t(d_attn, w_ref[3]).astype(BF)
        g_out = dot_o(mix_ref[...], d_attn).astype(BF)
        put(lambda i: g_out[i * part : (i + 1) * part], 3 * part, part)
        masks = head_masks(BF)

        def group(index, _):
            s, r, l = windows(index, groups)
            qs, ks, ds = (stacked(a[r, l], masks) for a in (q_ref, k_ref, dm_ref))
            probs = kernel_probabilities(qs, k_ref[r, l], valid_ref[pl.ds(s, 1)])
            d_probs = dot_t(ds, v_ref[r, l])
            dv_ref[r, l] = dot_o(probs.astype(BF), ds).astype(BF)
            d_scores = (probs * (d_probs - jnp.sum(probs * d_probs, axis=-1, keepdims=True))).astype(BF)
            dq_ref[r, l] = (dot(beside(d_scores), ks) * SCALE).astype(BF)
            dk_ref[r, l] = (dot_o(d_scores, qs) * SCALE).astype(BF)
            return 0

        lax.fori_loop(0, seqs * groups, group, 0)
        unit, inverse = layer_norm(rows_ref[...].astype(F32))
        normed = (unit * vec_ref[0:1] + vec_ref[1:2]).astype(BF)
        d_normed = dot_t(dq_ref[...], w_ref[0]) + dot_t(dk_ref[...], w_ref[1]) + dot_t(dv_ref[...], w_ref[2])
        dx_ref[...] = (dr_ref[...] + norm_back(d_normed, unit, inverse, vec_ref[0:1])).astype(BF)
        for n, ref in enumerate((dq_ref, dk_ref, dv_ref)):
            grad = dot_o(normed, ref[...]).astype(BF)
            put(lambda i: grad[i * part : (i + 1) * part], n * part, part)
        total = jnp.concatenate(
            [jnp.sum(a, axis=0, keepdims=True) for a in (d_normed * unit, d_normed)]
            + [jnp.sum(a[...].astype(F32), axis=0, keepdims=True) for a in (dq_ref, dv_ref)]
            + sums,
            axis=0,
        )
        put(lambda i: pltpu.roll(total, (width - i * part) % width, 1).astype(BF), 4 * part, 8)

    arrays = [branch, dn_own, dn_other, rows, q, k, v, mixed, residual, valid, matrices, vectors]
    return call(
        body,
        order,
        arrays,
        [whole(a.shape) for a in arrays],
        [((tokens, width), BF), ((2, slots, 4 * part + 8, width), BF)],
        [pltpu.VMEM((tokens, width), BF)] * 4 + [pltpu.VMEM((tokens, width), F32)],
        flops=16 * tokens * width * width,
        name="attention_backward",
    )


def feed_forward_kernel(order, pieces, normed_own, normed_other):
    slots = len(pieces)
    tokens, width = normed_own.shape
    half = (pieces[0].shape[0] - 8) // 2
    deep = half // 2
    hidden = slots * half
    tile = 256

    def body(order_ref, *refs):
        piece_refs = refs[:slots]
        own_ref, other_ref = refs[slots : slots + 2]
        inner, outer, act, slope_ref, p_own, p_other, small, bias, rows, sems = refs[slots + 2 :]
        copies = []
        for i, piece in enumerate(piece_refs):
            chip = order_ref[i]
            low = pl.multiple_of(chip * half, 8)
            row = pl.multiple_of(chip * deep, 8)
            copies.append(
                pltpu.make_async_copy(piece.at[pl.ds(0, half)], outer.at[pl.ds(low, half)], sems.at[i, 0])
            )
            copies.append(pltpu.make_async_copy(piece.at[pl.ds(half, 8)], small.at[chip], sems.at[i, 1]))
            for j in range(2):
                copies.append(
                    pltpu.make_async_copy(
                        piece.at[pl.ds(half + 8 + j * deep, deep)],
                        inner.at[pl.ds(row, deep), pl.ds(j * width, width)],
                        sems.at[i, 2 + j],
                    )
                )
        run_copies(copies)
        total = jnp.zeros((8, hidden), F32)
        for i in range(slots):
            wide = jnp.concatenate([small[i].astype(F32), jnp.zeros((8, hidden - width), F32)], axis=1)
            total = total + (pltpu.roll(wide, i * half, 1) if i else wide)
        bias[...] = total
        rows[0:tokens] = own_ref[...]
        rows[tokens:] = other_ref[...]

        def columns(index, _):
            cols = pl.ds(pl.multiple_of(index * tile, tile), tile)
            before = dot(rows[...], inner[:, cols]) + bias[0:1, cols]
            normal = 0.5 * (1.0 + lax.erf(before * (1.0 / math.sqrt(2.0))))
            slope = normal + before * jnp.exp(-0.5 * before * before) * (1.0 / math.sqrt(2.0 * math.pi))
            slope_ref[:, cols] = slope
            act[:, cols] = (before * normal).astype(BF)
            return 0

        lax.fori_loop(0, hidden // tile, columns, 0)
        partial = dot(act[...], outer[...])
        p_own[...] = partial[:tokens]
        p_other[...] = partial[tokens:].astype(BF)

    return call(
        body,
        order,
        list(pieces) + [normed_own, normed_other],
        [ANY] * slots + [whole(normed_own.shape)] * 2,
        [
            ((width, hidden), BF),
            ((hidden, width), BF),
            ((2 * tokens, hidden), BF),
            ((2 * tokens, hidden), F32),
            ((tokens, width), F32),
            ((tokens, width), BF),
        ],
        [
            pltpu.VMEM((slots, 8, width), BF),
            pltpu.VMEM((8, hidden), F32),
            pltpu.VMEM((2 * tokens, width), BF),
            pltpu.SemaphoreType.DMA((slots, 4)),
        ],
        flops=8 * tokens * width * hidden,
        name="feed_forward",
    )


def feed_forward_backward_kernel(order, branch_own, branch_other, normed_own, normed_other, kept):
    inner, outer, act, slope = kept
    tokens, width = branch_own.shape
    hidden = outer.shape[0]
    slots = order.shape[0]
    half = hidden // slots
    deep = half // 2
    tile = 256

    def body(
        order_ref, b_own, b_other, n_own, n_other, inner_ref, outer_ref, act_ref, slope_ref,
        g_ref, d_own, d_other, rows, branch, before, bias,
    ):
        rows[0:tokens] = n_own[...]
        rows[tokens:] = n_other[...]
        branch[0:tokens] = b_own[...]
        branch[tokens:] = b_other[...]

        def columns(index, _):
            cols = pl.ds(pl.multiple_of(index * tile, tile), tile)
            d_before = (dot_t(branch[...], outer_ref[cols, :]) * slope_ref[:, cols]).astype(BF)
            before[:, cols] = d_before
            bias[:, cols] = jnp.broadcast_to(jnp.sum(d_before.astype(F32), axis=0, keepdims=True), (8, tile))
            return 0

        lax.fori_loop(0, hidden // tile, columns, 0)
        d_normed = dot_t(before[...], inner_ref[...])
        d_own[...] = d_normed[:tokens]
        d_other[...] = d_normed[tokens:].astype(BF)
        g_outer = dot_o(act_ref[...], branch[...]).astype(BF)
        for i in range(slots):
            g_ref[order_ref[i], 0:half] = g_outer[i * half : (i + 1) * half]
        g_inner = dot_o(rows[...], before[...]).astype(BF)
        g_bias = bias[...]
        for i in range(slots):
            slot = order_ref[i]
            for j in range(2):
                low = half + 8 + j * deep
                g_ref[slot, low : low + deep] = g_inner[i * deep : (i + 1) * deep, j * width : (j + 1) * width]
            own = pltpu.roll(g_bias, hidden - i * half, 1) if i else g_bias
            g_ref[slot, half : half + 8] = own[:, :width].astype(BF)

    arrays = [branch_own, branch_other, normed_own, normed_other, inner, outer, act, slope]
    return call(
        body,
        order,
        arrays,
        [whole(a.shape) for a in arrays],
        [((slots, 2 * half + 8, width), BF), ((tokens, width), F32), ((tokens, width), BF)],
        [
            pltpu.VMEM((2 * tokens, width), BF),
            pltpu.VMEM((2 * tokens, width), BF),
            pltpu.VMEM((2 * tokens, hidden), BF),
            pltpu.VMEM((8, hidden), F32),
        ],
        flops=16 * tokens * width * hidden,
        name="feed_forward_backward",
    )


def fits(dp):
    return dp == 16


def column_pieces(piece):
    count = lax.axis_size("z")
    own = [piece]
    for k in range(1, count):
        own.append(lax.ppermute(piece, "z", [((i + k) % count, i) for i in range(count)]))
    return own + [swap(a, "x") for a in own]


def reduce_slots(keep, give):
    count = lax.axis_size("z")
    sums = [None] * count
    for t in list(range(1, count)) + [0]:
        sums[t] = (keep[t].astype(F32) + swap(give[t], "x").astype(F32)).astype(BF)
    total = sums[0].astype(F32)
    for t in range(1, count):
        total = total + lax.ppermute(sums[t], "z", [(i, (i + t) % count) for i in range(count)]).astype(F32)
    return total


def blocks(inputs, lengths, cotangent, *params):
    (
        ln1_gain,
        ln1_bias,
        w_query,
        b_query,
        w_key,
        w_value,
        b_value,
        w_out,
        b_out,
        ln2_gain,
        ln2_bias,
        w_inner,
        b_inner,
        w_outer,
        b_outer,
    ) = (a[0] for a in params)
    y, z, x, c = (lax.axis_index(name) for name in ("section", "z", "x", "core"))
    count = lax.axis_size("z")
    chips = count * 2
    seqs, length, width = inputs.shape
    tokens = seqs * length
    rows = w_query.shape[0]
    units = w_outer.shape[0]
    half = units // 2
    hidden = chips * half
    valid = (jnp.arange(length, dtype=jnp.int32)[None, :] < lengths[:, None]).astype(F32)
    row_valid = valid.reshape(tokens, 1)

    slot = jnp.arange(chips, dtype=jnp.int32)
    chip_of = lax.rem(z + lax.rem(slot, count), count) * 2 + jnp.bitwise_xor(x, slot // count)
    slot_of = jnp.bitwise_xor(x, lax.rem(slot, 2)) * count + lax.rem(slot // 2 + count - z, count)
    join_order = jnp.concatenate([2 * chip_of + c, 2 * chip_of + 1 - c])
    grad_order = jnp.concatenate([c[None], slot_of])

    small = jnp.stack([ln1_gain, ln1_bias, b_query, b_value, b_out, ln2_gain, ln2_bias, b_outer])
    small = jnp.pad(small, ((0, 0), (0, width - rows)))
    attention = column_pieces(jnp.concatenate([w_query, w_key, w_value, w_out, small]))
    matrices, vectors = join_attention(join_order, attention, swap(jnp.stack(attention), "core"))

    outer_halves = jnp.concatenate(
        [w_outer.reshape(2, half, width), jnp.pad(b_inner.reshape(2, 1, half), ((0, 0), (0, 7), (0, width - half)))],
        axis=1,
    )
    quarters = w_inner.reshape(rows, chips, 2, 2, half).transpose(3, 2, 0, 1, 4).reshape(2, 2, rows, 2, width)
    quarters = jnp.moveaxis(quarters, 3, 2)
    quarters = quarters.reshape(2, 4 * rows, width)
    packed = jnp.concatenate([outer_halves, quarters], axis=1)
    mine, other = pick(packed, y), swap(pick(packed, 1 - y), "section")
    both = pair(mine, other, y)
    inner_both = both[:, half + 8 :].reshape(2, 2, 2, rows, width)
    inner_mine = lax.dynamic_index_in_dim(inner_both, c, 1, keepdims=False)
    inner_other = swap(lax.dynamic_index_in_dim(inner_both, 1 - c, 1, keepdims=False), "core")
    inner_rows = jnp.moveaxis(pair(inner_mine, inner_other, c), 0, 2).reshape(2, 4 * rows, width)
    pieces = [
        column_pieces(jnp.concatenate([both[layer, : half + 8], inner_rows[layer]])) for layer in range(2)
    ]

    def spread(own, source):
        if source is not None:
            own = jnp.where(y == source, own, send(own, "section", source))
        return own, swap(own, "core")

    outputs, saved, ff_saved = [], [], []
    current = inputs.reshape(tokens, width)
    for layer in range(2):
        residual, normed_two, q, k, v, mixed = attention_forward_kernel(
            join_order, current, valid, matrices, vectors
        )
        saved.append((current, q, k, v, mixed, residual))
        normed = spread(normed_two, layer)
        *kept, part_own, part_other = feed_forward_kernel(chip_of, pieces[layer], *normed)
        ff_saved.append((normed, kept))
        own = part_own + swap(part_other, "core").astype(F32)
        own = jnp.where(y == layer, own + residual + vectors[7], own)
        current = ((own + swap(own.astype(BF), "section").astype(F32)) * row_valid).astype(BF)
        outputs.append(current)
    layer_out = jnp.where(y == 0, outputs[0], outputs[1])

    ff_grads, attention_grads, input_grads = [None, None], [None, None], [None, None]
    upstream = cotangent.reshape(tokens, width)
    for layer in (1, 0):
        branch = (upstream.astype(F32) * row_valid).astype(BF)
        branches = spread(branch, None if layer == 1 else 1)
        normed, kept = ff_saved[layer]
        grads, d_own, d_other = feed_forward_backward_kernel(slot_of, *branches, *normed, kept)
        ff_grads[layer] = reduce_slots(
            [grads[t] for t in range(count)], [grads[count + t] for t in range(count)]
        )
        d_own = d_own + swap(d_other, "core").astype(F32)
        d_section = send(d_own.astype(BF), "section", 1 - layer)
        upstream, attention_grads[layer] = attention_backward_kernel(
            grad_order, branches[0], d_own, d_section, saved[layer], valid, matrices, vectors, chips
        )
        input_grads[layer] = upstream
    input_grad = jnp.where(y == 0, input_grads[0], input_grads[1])

    grads = jnp.where(y == 0, *attention_grads)
    grads = (grads[0].astype(F32) + swap(grads[1], "core").astype(F32)).astype(BF)
    attention = reduce_slots([grads[t] for t in range(count)], [grads[count + t] for t in range(count)])
    g_query, g_key, g_value, g_out = (attention[k * rows : (k + 1) * rows] for k in range(4))
    g_small = attention[4 * rows :, :rows]

    sent = jnp.where(
        y == 0, send(ff_grads[0].astype(BF), "section", 1), send(ff_grads[1].astype(BF), "section", 0)
    ).astype(F32)
    home = pair(jnp.where(y == 0, *ff_grads), sent, y)
    g_outer = home[:, :half].reshape(units, width)
    g_bias = home[:, half, :half].reshape(units)
    halves = home[:, half + 8 :].reshape(2, 2, 2, rows, width)
    own = lax.dynamic_index_in_dim(halves, c, 2, keepdims=False)
    other = swap(lax.dynamic_index_in_dim(halves, 1 - c, 2, keepdims=False).astype(BF), "core").astype(F32)
    g_inner = pair(own, other, c).transpose(0, 1, 3, 2, 4).reshape(2, 2, rows, chips, half)
    g_inner = g_inner.transpose(2, 3, 0, 1, 4).reshape(rows, 2 * units * chips)
    return (
        layer_out.reshape(1, seqs, length, width),
        input_grad.reshape(1, seqs, length, width),
        g_small[0:1],
        g_small[1:2],
        g_query[None],
        g_small[2:3],
        g_key[None],
        g_value[None],
        g_small[3:4],
        g_out[None],
        g_small[4:5],
        g_small[5:6],
        g_small[6:7],
        g_inner[None],
        g_bias[None],
        g_outer[None],
        g_small[7:8],
    )


def solution(mesh):
    sections, dp = mesh.devices.shape
    fine = Mesh(mesh.devices.reshape(sections, dp // 4, 2, 2), ("section", "z", "x", "core"))
    rows = ("z", "x", "core")
    vector, matrix = P("section", rows), P("section", rows, None)
    stacked = P("section", rows, None, None)
    kinds = (
        vector, vector, matrix, vector, matrix, matrix, vector, matrix,
        vector, vector, vector, matrix, vector, matrix, vector,
    )
    return jax.shard_map(
        blocks if fits(dp) else per_device_general,
        mesh=fine,
        in_specs=(P(rows, None, None), P(rows), P(rows, None, None)) + kinds,
        out_specs=(stacked, stacked) + kinds,
        check_vma=False,
    )
```
